256 devices in a mesh: gx: 8 (over x, core), gy: 32 (over z, y).
Axes of the slice: x: 4, y: 4, z: 8, core: 2. Of those that a mesh axis runs over, the one named last changes fastest.
Arguments:
- old_heads: float32 [4, 1024, 4096], P(None, 'gx', 'gy'), may hold values from -6 to 6
- conductance_x: float32 [4, 1024, 4096], P(None, 'gx', 'gy'), may hold values from 7.6 to 10.4
- conductance_y: float32 [4, 1024, 4096], P(None, 'gx', 'gy'), may hold values from 7.6 to 10.4
- storage: float32 [4, 1024, 4096], P(None, 'gx', 'gy'), may hold values from 0.25 to 4
- sources: float32 [4, 1024, 4096], P(None, 'gx', 'gy'), may hold values from -6 to 6
- cotangent: float32 [4, 1024, 4096], P(None, 'gx', 'gy'), may hold values from -6 to 6
- active_mask: int32 [1024, 4096], P('gx', 'gy'), may hold values from 0 to 1, as said below
- layer_scale: float32 [64], replicated, may hold values from 0.5 to 2
- window_layers: int32 [4], replicated, may hold values from 0 to 63
Outputs:
- new_heads: float32 [4, 1024, 4096], P(None, 'gx', 'gy')
- grad_heads: float32 [4, 1024, 4096], P(None, 'gx', 'gy')
- sensitivity_x: float32 [4, 1024, 4096], P(None, 'gx', 'gy')
- sensitivity_y: float32 [4, 1024, 4096], P(None, 'gx', 'gy')
The draws below stay inside these ranges and needn't reach their ends.
Inputs may be any that keep to these rules, and one draw needn't show every extreme that they name: `active_mask`: 1 for an active column of cells, 0 for an inactive one.
All inputs are finite; a program needn't handle non-finite values.
Results may differ from the reference program's by a relative error of at most 0.0017.
Values sent between devices are 32-bit elements; how exact they have to be, the bound alone decides.
No kernel may reach another device: no remote copies, remote signals or barrier semaphores. Data moves between devices by JAX's collectives and lax.ppermute only.
A program may use at most 128 MiB of HBM per device.

```python
import math
import jax
import jax.numpy as jnp
from jax import lax

ALL_LAYERS = 64
LAYERS = 4
NX = 1024
NY = 4096


def draw_active_mask(key, part):
    keys = jax.random.split(key, 5)
    margin_y = max(NY // 16, 1)
    margin_x = max(NX // 16, 1)
    left_edge = jax.random.randint(keys[0], (NX, 1), 1, margin_y + 1)
    right_edge = NY - jax.random.randint(keys[1], (NX, 1), 1, margin_y + 1)
    top_edge = jax.random.randint(keys[2], (1, NY), 1, margin_x + 1)
    bottom_edge = NX - jax.random.randint(keys[3], (1, NY), 1, margin_x + 1)
    row_index = jnp.arange(NX, dtype=jnp.int32)[:, None]
    col_index = jnp.arange(NY, dtype=jnp.int32)[None, :]
    inside = (col_index >= left_edge) & (col_index < right_edge) & (row_index >= top_edge) & (row_index < bottom_edge)
    wells = jax.random.randint(keys[4], (NX, NY), 0, 1024) == 0
    return jnp.where(inside & jnp.logical_not(wells), 1, 0).astype(jnp.int32)


def touch_ends(values, own_key, low, top_value):
    index_at = [jax.random.randint(jax.random.fold_in(own_key, axis), (), 0, length) for axis, length in enumerate(values.shape)]
    longest = values.shape.index(max(values.shape))
    beside = index_at[:longest] + [(index_at[longest] + 1) % values.shape[longest]] + index_at[longest + 1:]
    return values.at[tuple(index_at)].set(low).at[tuple(beside)].set(top_value)


def block_levels(rng, extent, shards, smallest, largest):
    level = 1.0
    for position, shards_of in shards:
        draws = jax.random.uniform(jax.random.fold_in(jax.random.fold_in(rng, 6), position), (shards_of,), jnp.float32, smallest / len(shards), largest / len(shards))
        level = level * jnp.repeat(jnp.exp(draws), extent[position] // shards_of).reshape((-1,) + (1,) * (len(extent) - 1 - position))
    return level


def normal_values(rng, shape, scale, most, cuts=(), kind=jnp.bfloat16):
    values = jax.random.normal(rng, shape, jnp.float32) * scale
    if len(cuts) > 0:
        values = block_levels(rng, shape, cuts, -0.22, 0.18) * values
    return jnp.clip(values, min=-most, max=most).astype(kind)


def setup_inputs(seed: int = 0) -> dict:
    seeds = jax.random.split(jax.random.key(seed), 10)
    return {
        "old_heads": normal_values(seeds[0], (LAYERS, NX, NY), 1.0, 6.0, ((1, 8), (2, 32)), jnp.float32),
        "conductance_x": jnp.clip(7.6 + 2.7999997 * jax.random.uniform(seeds[1], (LAYERS, NX, NY), jnp.float32) ** block_levels(seeds[1], (LAYERS, NX, NY), ((1, 8), (2, 32)), -0.2, 0.2), 7.6, 10.4),
        "conductance_y": jnp.clip(7.6 + 2.7999997 * jax.random.uniform(seeds[2], (LAYERS, NX, NY), jnp.float32) ** block_levels(seeds[2], (LAYERS, NX, NY), ((1, 8), (2, 32)), -0.2, 0.2), 7.6, 10.4),
        "storage": jnp.clip(jnp.exp(math.log(4.0) - 2.7725887 * jax.random.uniform(seeds[3], (LAYERS, NX, NY), jnp.float32) ** block_levels(seeds[3], (LAYERS, NX, NY), ((1, 8), (2, 32)), -0.2, 0.2)), 0.25, 4.0),
        "sources": normal_values(seeds[4], (LAYERS, NX, NY), 1.0, 6.0, ((1, 8), (2, 32)), jnp.float32),
        "cotangent": normal_values(seeds[5], (LAYERS, NX, NY), 1.0, 6.0, ((1, 8), (2, 32)), jnp.float32),
        "active_mask": draw_active_mask(jax.random.fold_in(seeds[9], 71), 0),
        "layer_scale": jnp.clip(jnp.exp(jax.random.uniform(seeds[7], (ALL_LAYERS,), jnp.float32, math.log(0.5), math.log(2.0))), 0.5, 2.0),
        "window_layers": touch_ends(jax.random.randint(seeds[8], (LAYERS,), 0, ALL_LAYERS), jax.random.fold_in(seeds[8], 1), 0, ALL_LAYERS - 1).astype(jnp.int32),
    }


def layer_weights(layer_scale, window_layers):
    matches = window_layers[:, None] == jnp.arange(layer_scale.shape[0], dtype=jnp.int32)[None, :]
    return jnp.sum(jnp.where(matches, layer_scale[None, :], jnp.float32(0.0)), axis=1)


def next_along(values, line_axis):
    length = values.shape[line_axis]
    rest = lax.slice_in_dim(values, 1, length, axis=line_axis)
    filler = jnp.zeros_like(lax.slice_in_dim(values, 0, 1, axis=line_axis))
    return jnp.concatenate([rest, filler], axis=line_axis)


def prev_along(values, line_axis):
    length = values.shape[line_axis]
    rest = lax.slice_in_dim(values, 0, length - 1, axis=line_axis)
    filler = jnp.zeros_like(lax.slice_in_dim(values, 0, 1, axis=line_axis))
    return jnp.concatenate([filler, rest], axis=line_axis)


def thomas(lower_band, diag_band, upper_band, right_side):
    zeros_row = jnp.zeros_like(right_side[0])

    def downward(state, entries):
        pivot_prev, partial_prev = state
        lower_now, diag_now, upper_now, rhs_now = entries
        denom = diag_now - lower_now * pivot_prev
        pivot_now = upper_now / denom
        partial_now = (rhs_now - lower_now * partial_prev) / denom
        return (pivot_now, partial_now), (pivot_now, partial_now)

    unused, (pivots, partials) = lax.scan(downward, (zeros_row, zeros_row), (lower_band, diag_band, upper_band, right_side))

    def upward(later, entries):
        pivot_now, partial_now = entries
        value_now = partial_now - pivot_now * later
        return value_now, value_now

    unused_last, solved = lax.scan(upward, zeros_row, (pivots, partials), reverse=True)
    return solved


def line_solve(faces, storage, right_side, line_axis):
    after = jnp.moveaxis(faces, line_axis, 0)
    store_moved = jnp.moveaxis(storage, line_axis, 0)
    rhs_moved = jnp.moveaxis(right_side, line_axis, 0)
    before = prev_along(after, 0)
    solved = thomas(-before, store_moved + before + after, -after, rhs_moved)
    return jnp.moveaxis(solved, 0, line_axis)


def reference(old_heads, conductance_x, conductance_y, storage, sources, cotangent, active_mask, layer_scale, window_layers):
    active = active_mask.astype(jnp.float32)
    weight = layer_weights(layer_scale, window_layers)[:, None, None]
    xfaces = jnp.exp(conductance_x) * weight * (active * next_along(active, 0))[None]
    yfaces = jnp.exp(conductance_y) * weight * (active * next_along(active, 1))[None]
    mid_heads = line_solve(xfaces, storage, storage * old_heads + sources, 1)
    new_heads = line_solve(yfaces, storage, storage * mid_heads, 2)
    adjoint_y = line_solve(yfaces, storage, cotangent, 2)
    adjoint_x = line_solve(xfaces, storage, storage * adjoint_y, 1)
    grad_heads = storage * adjoint_x
    sensitivity_x = -xfaces * (adjoint_x - next_along(adjoint_x, 1)) * (mid_heads - next_along(mid_heads, 1))
    sensitivity_y = -yfaces * (adjoint_y - next_along(adjoint_y, 2)) * (new_heads - next_along(new_heads, 2))
    return new_heads, grad_heads, sensitivity_x, sensitivity_y
```

```python
import functools

import jax
import jax.numpy as jnp
from jax import lax
from jax.experimental import pallas as pl
from jax.experimental.pallas import tpu as pltpu
from jax.sharding import PartitionSpec as P

STEPS = 64
SLAB = (8, 128)
F32 = jnp.float32
VMEM = pl.BlockSpec(memory_space=pltpu.VMEM)
SMEM = pl.BlockSpec(memory_space=pltpu.SMEM)


def even_rows():
    return lax.rem(lax.broadcasted_iota(jnp.int32, SLAB, 0), 2) == 0


def down(slab):
    return pltpu.roll(slab, 7, 0)


def up(slab):
    return pltpu.roll(slab, 1, 0)


def mixed(even, first, second):
    return jnp.where(even, first, up(second))


def rows(t):
    return pl.ds(t, 8, stride=STEPS)


def plus(a, b):
    if a is None:
        return b
    return a if b is None else a + b


def reduce_all(lo, hi, face, store, right, keep):
    if hi == lo + 1:
        return face(lo), None, None, None, None
    mid = (lo + hi) // 2
    c_lo, s_lo, s_a, r_lo, r_a = reduce_all(lo, mid, face, store, right, keep)
    c_hi, s_b, s_hi, r_b, r_hi = reduce_all(mid, hi, face, store, right, keep)
    held = plus(store(mid), plus(s_a, s_b))
    load = plus(right(mid), plus(r_a, r_b))
    inv = 1.0 / (held + (c_lo + c_hi))
    to_lo = c_lo * inv
    to_hi = c_hi * inv
    keep(mid, to_lo, to_hi, inv, load * inv)
    return (
        to_lo * c_hi,
        plus(s_lo, to_lo * held),
        plus(s_hi, to_hi * held),
        plus(r_lo, to_lo * load),
        plus(r_hi, to_hi * load),
    )


def reduce_right(lo, hi, right, factor, keep):
    if hi == lo + 1:
        return None, None
    mid = (lo + hi) // 2
    r_lo, r_a = reduce_right(lo, mid, right, factor, keep)
    r_b, r_hi = reduce_right(mid, hi, right, factor, keep)
    load = plus(right(mid), plus(r_a, r_b))
    to_lo, to_hi, inv = factor(mid)
    keep(mid, load * inv)
    return plus(r_lo, to_lo * load), plus(r_hi, to_hi * load)


def back(lo, hi, v_lo, v_hi, factor, emit):
    if hi == lo + 1:
        return
    mid = (lo + hi) // 2
    to_lo, to_hi, part = factor(mid)
    value = part + to_lo * v_lo + to_hi * v_hi
    emit(mid, value)
    back(lo, mid, v_lo, value, factor, emit)
    back(mid, hi, value, v_hi, factor, emit)


def weights(scale_ref, window_ref):
    layer = lax.broadcasted_iota(jnp.int32, SLAB, 0) // 2
    weight = jnp.full(SLAB, scale_ref[window_ref[0]], F32)
    for l in range(1, 4):
        weight = jnp.where(layer == l, scale_ref[window_ref[l]], weight)
    return weight


def condense(cond, store, right, active_ref, weight, copies, outs):
    face_ref, store_ref, lo_ref, hi_ref, inv_ref, part_ref, pay_ref = outs
    even = even_rows()
    first_active = active_ref[rows(0), :]

    def active(t):
        if t < STEPS:
            return active_ref[rows(t), :]
        return jnp.where(even, down(first_active), 1.0)

    def face(t):
        value = jnp.exp(cond(t)) * weight * (active(t) * active(t + 1))
        face_ref[t] = value
        return value

    def held(t):
        value = store(t)
        store_ref[t] = value
        return value

    def keep(t, to_lo, to_hi, inv, part):
        lo_ref[t] = to_lo
        hi_ref[t] = to_hi
        inv_ref[t] = inv
        part_ref[t] = part

    last = STEPS - 1
    s_0, s_63 = held(0), held(last)
    r_0, r_63 = right(0), right(last)
    c, ds_0, ds_63, dr_0, dr_63 = reduce_all(0, last, face, held, right, keep)
    s_0, s_63, r_0, r_63 = s_0 + ds_0, s_63 + ds_63, r_0 + dr_0, r_63 + dr_63
    middle = face(last)
    c_two, s_64, s_127 = down(c), down(s_0), down(s_63)
    r_64, r_127 = down(r_0), down(r_63)
    inv = 1.0 / (s_63 + (c + middle))
    a, b = c * inv, middle * inv
    keep(0, a, b, inv, r_63 * inv)
    c = a * middle
    s_0, s_64, r_0, r_64 = s_0 + a * s_63, s_64 + b * s_63, r_0 + a * r_63, r_64 + b * r_63
    inv = 1.0 / (s_64 + (c + c_two))
    a, b = c * inv, c_two * inv
    keep(last, a, b, inv, r_64 * inv)
    c = a * c_two
    s_0, s_127, r_0, r_127 = s_0 + a * s_64, s_127 + b * s_64, r_0 + a * r_64, r_127 + b * r_64
    payload = (
        mixed(even, s_0, s_127),
        mixed(even, r_0, r_127),
        jnp.where(even, c, middle),
        jnp.where(even, first_active, 0.0),
    )
    for k in range(copies):
        for v, slab in enumerate(payload):
            pay_ref[pl.ds(32 * k + 8 * v, 8), :] = slab


def condense_right(right, factors, part_ref, pay_ref, copies):
    lo_ref, hi_ref, inv_ref = factors
    even = even_rows()

    def keep(t, part):
        part_ref[t] = part

    last = STEPS - 1
    dr_0, dr_63 = reduce_right(
        0, last, right, lambda t: (lo_ref[t], hi_ref[t], inv_ref[t]), keep
    )
    r_0, r_63 = right(0) + dr_0, right(last) + dr_63
    r_64, r_127 = down(r_0), down(r_63)
    part_ref[0] = r_63 * inv_ref[0]
    r_0, r_64 = r_0 + lo_ref[0] * r_63, r_64 + hi_ref[0] * r_63
    part_ref[last] = r_64 * inv_ref[last]
    r_0, r_127 = r_0 + lo_ref[last] * r_64, r_127 + hi_ref[last] * r_64
    slab = mixed(even, r_0, r_127)
    for k in range(copies):
        pay_ref[pl.ds(8 * k, 8), :] = slab


def chain_all(got_ref, count, factors, value_ref, link_ref):
    lo_ref, hi_ref, inv_ref = factors
    end = 2 * count - 1

    def slab(m, v):
        return got_ref[pl.ds(32 * m + 8 * v, 8), :]

    def both(n, v):
        value = slab(n // 2, v)
        return value if n % 2 == 0 else down(value)

    def face(n):
        if n % 2 == 0:
            return slab(n // 2, 2)
        value = down(slab(n // 2, 2)) * slab(n // 2 + 1, 3)
        link_ref[n // 2] = value
        return value

    def keep(n, to_lo, to_hi, inv, part):
        lo_ref[n] = to_lo
        hi_ref[n] = to_hi
        inv_ref[n] = inv
        value_ref[n] = part

    c, ds_0, ds_n, dr_0, dr_n = reduce_all(
        0, end, face, lambda n: both(n, 0), lambda n: both(n, 1), keep
    )
    link_ref[count - 1] = jnp.zeros(SLAB, F32)
    s_0, s_n = both(0, 0) + ds_0, both(end, 0) + ds_n
    r_0, r_n = both(0, 1) + dr_0, both(end, 1) + dr_n
    inv_0 = 1.0 / (s_0 + c)
    to_n = c * inv_0
    inv_n = 1.0 / (s_n + to_n * s_0)
    hi_ref[0] = to_n
    inv_ref[0] = inv_0
    inv_ref[end] = inv_n
    v_n = (r_n + to_n * r_0) * inv_n
    v_0 = r_0 * inv_0 + to_n * v_n
    chain_back(count, factors, value_ref, v_0, v_n)


def chain_right(got_ref, count, factors, value_ref):
    lo_ref, hi_ref, inv_ref = factors
    end = 2 * count - 1

    def right(n):
        value = got_ref[pl.ds(8 * (n // 2), 8), :]
        return value if n % 2 == 0 else down(value)

    def keep(n, part):
        value_ref[n] = part

    dr_0, dr_n = reduce_right(
        0, end, right, lambda n: (lo_ref[n], hi_ref[n], inv_ref[n]), keep
    )
    r_0, r_n = right(0) + dr_0, right(end) + dr_n
    v_n = (r_n + hi_ref[0] * r_0) * inv_ref[end]
    v_0 = r_0 * inv_ref[0] + hi_ref[0] * v_n
    chain_back(count, factors, value_ref, v_0, v_n)


def chain_back(count, factors, value_ref, v_0, v_n):
    lo_ref, hi_ref, _ = factors
    end = 2 * count - 1

    def emit(n, value):
        value_ref[n] = value

    emit(0, v_0)
    emit(end, v_n)
    back(0, end, v_0, v_n, lambda n: (lo_ref[n], hi_ref[n], value_ref[n]), emit)


def expand(place, count, value_ref, factors, part_ref, emit):
    lo_ref, hi_ref, _ = factors
    even = even_rows()
    last = STEPS - 1
    u_0 = value_ref[2 * place]
    u_127 = value_ref[2 * place + 1]
    u_next = value_ref[jnp.minimum(2 * place + 2, 2 * count - 1)]
    v_64 = part_ref[last] + lo_ref[last] * u_0 + hi_ref[last] * u_127
    v_63 = part_ref[0] + lo_ref[0] * u_0 + hi_ref[0] * v_64
    v_first = mixed(even, u_0, v_64)
    v_last = mixed(even, v_63, u_127)
    emit(0, v_first)
    emit(last, v_last)
    emit(STEPS, mixed(even, v_64, u_next))
    back(0, last, v_first, v_last, lambda t: (lo_ref[t], hi_ref[t], part_ref[t]), emit)


def transpose_layers(src_ref, dst_ref, f=lambda x: x):
    for l in range(4):
        dst_ref[pl.ds(128 * l, 128), :] = f(src_ref[pl.ds(128 * l, 128), :]).T


def condense_x_kernel(copies, scale, window, heads, cond, store, source, active, *refs):
    *outs, act4 = refs
    value = active[...].astype(F32)
    for l in range(4):
        act4[pl.ds(128 * l, 128), :] = value
    condense(
        lambda t: cond[rows(t), :],
        lambda t: store[rows(t), :],
        lambda t: store[rows(t), :] * heads[rows(t), :] + source[rows(t), :],
        act4,
        weights(scale, window),
        copies,
        outs,
    )


def condense_y_kernel(copies, scale, window, cotangent, cond, store, active, *refs):
    *outs, act4, cond_t, store_t, cot_t = refs
    value = active[...].astype(F32).T
    for l in range(4):
        act4[pl.ds(128 * l, 128), :] = value
    transpose_layers(cond, cond_t)
    transpose_layers(store, store_t)
    transpose_layers(cotangent, cot_t)
    condense(
        lambda t: cond_t[rows(t), :],
        lambda t: store_t[rows(t), :],
        lambda t: cot_t[rows(t), :],
        act4,
        weights(scale, window),
        copies,
        outs,
    )


def middle_kernel(axis, count, copies, got, *refs):
    own, other = refs[0:3], refs[4:7]
    part, store = refs[3], refs[7]
    chain_out = refs[8:11]
    link_out, field_out, part_out, pay_out = refs[11:15]
    value, links, plain, turned = refs[15:19]
    place = lax.axis_index(axis)
    even = even_rows()
    chain_all(got, count, chain_out, value, links)
    link_out[...] = links[place]

    def emit(t, slab):
        field_out[t] = slab
        if t < STEPS:
            plain[rows(t), :] = store[t] * slab

    expand(place, count, value, own, part, emit)
    transpose_layers(plain, turned)
    condense_right(lambda t: turned[rows(t), :], other, part_out, pay_out, copies)


def sensitivity(face, link, first, second, put):
    even = even_rows()
    for t in range(STEPS):
        value = face[t]
        if t == STEPS - 1:
            value = mixed(even, value, link[...])
        put(t, -value * (first[t] - first[t + 1]) * (second[t] - second[t + 1]))


def final_y_kernel(axis, count, got, *refs):
    chain, own = refs[0:3], refs[3:6]
    part, face, link, adjoint, heads_out, sens_out, value, field, plain, plain2 = refs[6:16]
    place = lax.axis_index(axis)
    chain_right(got, count, chain, value)

    def emit(t, slab):
        field[t] = slab
        if t < STEPS:
            plain[rows(t), :] = slab

    def put(t, slab):
        plain2[rows(t), :] = slab

    expand(place, count, value, own, part, emit)
    transpose_layers(plain, heads_out)
    sensitivity(face, link, adjoint, field, put)
    transpose_layers(plain2, sens_out)


def final_x_kernel(axis, count, got, *refs):
    chain, own = refs[0:3], refs[3:6]
    part, face, store, link, mid, grad_out, sens_out, value, field = refs[6:15]
    place = lax.axis_index(axis)
    chain_right(got, count, chain, value)

    def emit(t, slab):
        field[t] = slab
        if t < STEPS:
            grad_out[rows(t), :] = store[t] * slab

    def put(t, slab):
        sens_out[rows(t), :] = slab

    expand(place, count, value, own, part, emit)
    sensitivity(face, link, field, mid, put)


def shaped(*shape):
    return jax.ShapeDtypeStruct(shape, F32)


SLABS = shaped(STEPS, *SLAB)
TALL = shaped(STEPS + 1, *SLAB)
PLAIN = shaped(512, 128)


def call(kernel, name, args, outs, scratch, scalars=0):
    return pl.pallas_call(
        kernel,
        name=name,
        out_shape=tuple(outs),
        in_specs=[SMEM] * scalars + [VMEM] * (len(args) - scalars),
        out_specs=tuple([VMEM] * len(outs)),
        scratch_shapes=[pltpu.VMEM(s.shape, F32) for s in scratch],
        cost_estimate=pl.CostEstimate(flops=4000000, bytes_accessed=4000000, transcendentals=0),
        compiler_params=pltpu.CompilerParams(vmem_limit_bytes=16 * 1024 * 1024),
    )(*args)


def spread(payload, axis):
    return lax.all_to_all(payload, axis, split_axis=0, concat_axis=0, tiled=True)


def on_device(heads, cond_x, cond_y, store, source, cotangent, active, scale, window):
    nx, ny = lax.axis_size("gx"), lax.axis_size("gy")
    heads, cond_x, cond_y, store, source, cotangent = (
        a.reshape(512, 128) for a in (heads, cond_x, cond_y, store, source, cotangent)
    )
    kept = [SLABS] * 6
    *x_kept, pay_x = call(
        functools.partial(condense_x_kernel, nx),
        "condense_x",
        (scale, window, heads, cond_x, store, source, active),
        kept + [shaped(32 * nx, 128)],
        [PLAIN],
        2,
    )
    x_face, x_store, *x_own, x_part = x_kept
    got_x = spread(pay_x, "gx")
    *y_kept, pay_y = call(
        functools.partial(condense_y_kernel, ny),
        "condense_y",
        (scale, window, cotangent, cond_y, store, active),
        kept + [shaped(32 * ny, 128)],
        [PLAIN] * 4,
        2,
    )
    y_face, y_store, *y_own, y_part = y_kept
    got_y = spread(pay_y, "gy")

    def middle(axis, count, copies, name, got, own, part, other, kept_store):
        nodes = shaped(2 * count, *SLAB)
        *chain, link, field, part_new, pay = call(
            functools.partial(middle_kernel, axis, count, copies),
            name,
            (got, *own, part, *other, kept_store),
            [nodes] * 3 + [shaped(*SLAB), TALL, SLABS, shaped(8 * copies, 128)],
            [nodes, shaped(count, *SLAB), PLAIN, PLAIN],
        )
        return chain, link, field, part_new, pay

    x_chain, x_link, mid, y_part_new, pay_y2 = middle(
        "gx", nx, ny, "middle_x", got_x, x_own, x_part, y_own, x_store
    )
    got_y2 = spread(pay_y2, "gy")
    y_chain, y_link, adjoint_y, x_part_new, pay_x2 = middle(
        "gy", ny, nx, "middle_y", got_y, y_own, y_part, x_own, y_store
    )
    got_x2 = spread(pay_x2, "gx")
    new_heads, sens_y = call(
        functools.partial(final_y_kernel, "gy", ny),
        "final_y",
        (got_y2, *y_chain, *y_own, y_part_new, y_face, y_link, adjoint_y),
        [PLAIN] * 2,
        [shaped(2 * ny, *SLAB), TALL, PLAIN, PLAIN],
    )
    grad, sens_x = call(
        functools.partial(final_x_kernel, "gx", nx),
        "final_x",
        (got_x2, *x_chain, *x_own, x_part_new, x_face, x_store, x_link, mid),
        [PLAIN] * 2,
        [shaped(2 * nx, *SLAB), TALL],
    )
    return tuple(a.reshape(4, 128, 128) for a in (new_heads, grad, sens_x, sens_y))


def solution(mesh):
    field = P(None, "gx", "gy")
    return jax.shard_map(
        on_device,
        mesh=mesh,
        in_specs=(field,) * 6 + (P("gx", "gy"), P(), P()),
        out_specs=(field,) * 4,
        check_vma=False,
    )
```

```python
import functools

import jax
import jax.numpy as jnp
from jax import lax
from jax.experimental import pallas as pl
from jax.experimental.pallas import tpu as pltpu
from jax.sharding import PartitionSpec as P

STEPS = 64
SLAB = (8, 128)
F32 = jnp.float32
HBM = pl.BlockSpec(memory_space=pltpu.HBM)


def even_rows():
    return lax.rem(lax.broadcasted_iota(jnp.int32, SLAB, 0), 2) == 0


def down(slab):
    return pltpu.roll(slab, 7, 0)


def up(slab):
    return pltpu.roll(slab, 1, 0)


def mixed(even, first, second):
    return jnp.where(even, first, up(second))


def rows(t):
    return pl.ds(t, 8, stride=STEPS)


def plus(a, b):
    if a is None:
        return b
    return a if b is None else a + b


def join(mid, left, right_part, store, right, keep):
    c_lo, s_lo, s_a, r_lo, r_a = left
    c_hi, s_b, s_hi, r_b, r_hi = right_part
    held = plus(store(mid), plus(s_a, s_b))
    load = plus(right(mid), plus(r_a, r_b))
    inv = 1.0 / (held + (c_lo + c_hi))
    to_lo = c_lo * inv
    to_hi = c_hi * inv
    keep(mid, to_lo, to_hi, inv, load * inv)
    return (
        to_lo * c_hi,
        plus(s_lo, to_lo * held),
        plus(s_hi, to_hi * held),
        plus(r_lo, to_lo * load),
        plus(r_hi, to_hi * load),
    )


def reduce_all(lo, hi, face, store, right, keep):
    if hi == lo + 1:
        return face(lo), None, None, None, None
    mid = (lo + hi) // 2
    left = reduce_all(lo, mid, face, store, right, keep)
    return join(mid, left, reduce_all(mid, hi, face, store, right, keep), store, right, keep)


def reduce_right(lo, hi, right, factor, keep):
    if hi == lo + 1:
        return None, None
    mid = (lo + hi) // 2
    r_lo, r_a = reduce_right(lo, mid, right, factor, keep)
    r_b, r_hi = reduce_right(mid, hi, right, factor, keep)
    load = plus(right(mid), plus(r_a, r_b))
    to_lo, to_hi, inv = factor(mid)
    keep(mid, load * inv)
    return plus(r_lo, to_lo * load), plus(r_hi, to_hi * load)


def back(lo, hi, v_lo, v_hi, factor, emit):
    if hi == lo + 1:
        return
    mid = (lo + hi) // 2
    to_lo, to_hi, part = factor(mid)
    value = part + to_lo * v_lo + to_hi * v_hi
    emit(mid, value)
    back(lo, mid, v_lo, value, factor, emit)
    back(mid, hi, value, v_hi, factor, emit)


def weights(scale_ref, window_ref):
    layer = lax.broadcasted_iota(jnp.int32, SLAB, 0) // 2
    weight = jnp.full(SLAB, scale_ref[window_ref[0]], F32)
    for l in range(1, 4):
        weight = jnp.where(layer == l, scale_ref[window_ref[l]], weight)
    return weight


HALF = (STEPS - 1) // 2
FACE, STORE, INV, LO, HI, PART = range(6)


def condense(cond, store, right, active_ref, weight, copies, kept, kept_h, pay, pay_h, sems):
    even = even_rows()
    first_active = active_ref[rows(0), :]

    def active(t):
        if t < STEPS:
            return active_ref[rows(t), :]
        return jnp.where(even, down(first_active), 1.0)

    def face(t):
        value = jnp.exp(cond(t)) * weight * (active(t) * active(t + 1))
        kept[FACE, t] = value
        return value

    def held(t):
        value = store(t)
        kept[STORE, t] = value
        return value

    def keep(t, to_lo, to_hi, inv, part):
        kept[LO, t] = to_lo
        kept[HI, t] = to_hi
        kept[INV, t] = inv
        kept[PART, t] = part

    last = STEPS - 1
    s_0, s_63 = held(0), held(last)
    r_0, r_63 = right(0), right(last)
    left = reduce_all(0, HALF, face, held, right, keep)
    early = pltpu.make_async_copy(
        kept.at[:, pl.ds(1, HALF - 1)], kept_h.at[:, pl.ds(1, HALF - 1)], sems.at[0]
    )
    early.start()
    c, ds_0, ds_63, dr_0, dr_63 = join(
        HALF, left, reduce_all(HALF, last, face, held, right, keep), held, right, keep
    )
    s_0, s_63, r_0, r_63 = s_0 + ds_0, s_63 + ds_63, r_0 + dr_0, r_63 + dr_63
    middle = face(last)
    c_two, s_64, s_127 = down(c), down(s_0), down(s_63)
    r_64, r_127 = down(r_0), down(r_63)
    inv = 1.0 / (s_63 + (c + middle))
    a, b = c * inv, middle * inv
    keep(last, a, b, inv, r_63 * inv)
    c = a * middle
    s_0, s_64, r_0, r_64 = s_0 + a * s_63, s_64 + b * s_63, r_0 + a * r_63, r_64 + b * r_63
    inv = 1.0 / (s_64 + (c + c_two))
    a, b = c * inv, c_two * inv
    keep(STEPS, a, b, inv, r_64 * inv)
    c = a * c_two
    s_0, s_127, r_0, r_127 = s_0 + a * s_64, s_127 + b * s_64, r_0 + a * r_64, r_127 + b * r_64
    payload = (
        mixed(even, s_0, s_127),
        mixed(even, r_0, r_127),
        jnp.where(even, c, middle),
        jnp.where(even, first_active, 0.0),
    )
    for k in range(copies):
        for v, slab in enumerate(payload):
            pay[pl.ds(32 * k + 8 * v, 8), :] = slab
    sends = [
        pltpu.make_async_copy(pay, pay_h, sems.at[1]),
        pltpu.make_async_copy(
            kept.at[:, pl.ds(HALF, TALL_STEPS - HALF)],
            kept_h.at[:, pl.ds(HALF, TALL_STEPS - HALF)],
            sems.at[2],
        ),
        pltpu.make_async_copy(kept.at[:, 0], kept_h.at[:, 0], sems.at[3]),
    ]
    for send in sends:
        send.start()
    early.wait()
    for send in sends:
        send.wait()


def condense_right(right, factors, part_ref, pay_ref, copies):
    lo_ref, hi_ref, inv_ref = factors
    even = even_rows()

    def keep(t, part):
        part_ref[t] = part

    last = STEPS - 1
    dr_0, dr_63 = reduce_right(
        0, last, right, lambda t: (lo_ref[t], hi_ref[t], inv_ref[t]), keep
    )
    r_0, r_63 = right(0) + dr_0, right(last) + dr_63
    r_64, r_127 = down(r_0), down(r_63)
    part_ref[last] = r_63 * inv_ref[last]
    r_0, r_64 = r_0 + lo_ref[last] * r_63, r_64 + hi_ref[last] * r_63
    part_ref[STEPS] = r_64 * inv_ref[STEPS]
    r_0, r_127 = r_0 + lo_ref[STEPS] * r_64, r_127 + hi_ref[STEPS] * r_64
    slab = mixed(even, r_0, r_127)
    for k in range(copies):
        pay_ref[pl.ds(8 * k, 8), :] = slab


def chain_all(got_ref, count, size, factors, value_ref, link_ref):
    lo_ref, hi_ref, inv_ref = (factors.at[i] for i in range(3))
    end = 2 * count - 1

    def slab(m, v):
        return got_ref[pl.ds(size * m + 8 * v, 8), :]

    def both(n, v):
        value = slab(n // 2, v)
        return value if n % 2 == 0 else down(value)

    def face(n):
        if n % 2 == 0:
            return slab(n // 2, 2)
        value = down(slab(n // 2, 2)) * slab(n // 2 + 1, 3)
        link_ref[n // 2] = value
        return value

    def keep(n, to_lo, to_hi, inv, part):
        lo_ref[n] = to_lo
        hi_ref[n] = to_hi
        inv_ref[n] = inv
        value_ref[n] = part

    c, ds_0, ds_n, dr_0, dr_n = reduce_all(
        0, end, face, lambda n: both(n, 0), lambda n: both(n, 1), keep
    )
    link_ref[count - 1] = jnp.zeros(SLAB, F32)
    s_0, s_n = both(0, 0) + ds_0, both(end, 0) + ds_n
    r_0, r_n = both(0, 1) + dr_0, both(end, 1) + dr_n
    inv_0 = 1.0 / (s_0 + c)
    to_n = c * inv_0
    inv_n = 1.0 / (s_n + to_n * s_0)
    hi_ref[0] = to_n
    inv_ref[0] = inv_0
    inv_ref[end] = inv_n
    v_n = (r_n + to_n * r_0) * inv_n
    v_0 = r_0 * inv_0 + to_n * v_n
    chain_back(count, factors, value_ref, v_0, v_n)


def chain_right(got_ref, count, factors, value_ref):
    lo_ref, hi_ref, inv_ref = (factors.at[i] for i in range(3))
    end = 2 * count - 1

    def right(n):
        value = got_ref[pl.ds(8 * (n // 2), 8), :]
        return value if n % 2 == 0 else down(value)

    def keep(n, part):
        value_ref[n] = part

    dr_0, dr_n = reduce_right(
        0, end, right, lambda n: (lo_ref[n], hi_ref[n], inv_ref[n]), keep
    )
    r_0, r_n = right(0) + dr_0, right(end) + dr_n
    v_n = (r_n + hi_ref[0] * r_0) * inv_ref[end]
    v_0 = r_0 * inv_ref[0] + hi_ref[0] * v_n
    chain_back(count, factors, value_ref, v_0, v_n)


def chain_back(count, factors, value_ref, v_0, v_n):
    lo_ref, hi_ref = factors.at[0], factors.at[1]
    end = 2 * count - 1

    def emit(n, value):
        value_ref[n] = value

    emit(0, v_0)
    emit(end, v_n)
    back(0, end, v_0, v_n, lambda n: (lo_ref[n], hi_ref[n], value_ref[n]), emit)


def expand(place, count, value_ref, factors, part_ref, emit):
    lo_ref, hi_ref = factors
    even = even_rows()
    last = STEPS - 1
    u_0 = value_ref[2 * place]
    u_127 = value_ref[2 * place + 1]
    u_next = value_ref[jnp.minimum(2 * place + 2, 2 * count - 1)]
    v_64 = part_ref[STEPS] + lo_ref[STEPS] * u_0 + hi_ref[STEPS] * u_127
    v_63 = part_ref[last] + lo_ref[last] * u_0 + hi_ref[last] * v_64
    v_first = mixed(even, u_0, v_64)
    v_last = mixed(even, v_63, u_127)
    emit(0, v_first)
    emit(last, v_last)
    emit(STEPS, mixed(even, v_64, u_next))
    back(0, last, v_first, v_last, lambda t: (lo_ref[t], hi_ref[t], part_ref[t]), emit)


def transpose_layers(src_ref, dst_ref, f=lambda x: x):
    for l in range(4):
        dst_ref[pl.ds(128 * l, 128), :] = f(src_ref[pl.ds(128 * l, 128), :]).T


class Copies:
    def __init__(self, sems, first, pairs):
        self.copies = [
            pltpu.make_async_copy(src, dst, sems.at[first + i])
            for i, (src, dst) in enumerate(pairs)
        ]
        for copy in self.copies:
            copy.start()

    def wait(self, *indices):
        for i in indices:
            self.copies[i].wait()


def condense_x_kernel(
    copies, scale_h, window_h, heads_h, cond_h, store_h, source_h, active_h, order_h,
    kept_h, pay_h,
    scale, window, heads, cond, store, source, active, act4, kept, pay, sems,
):
    loads = Copies(
        sems,
        0,
        [
            (scale_h, scale), (window_h, window), (active_h, active), (cond_h, cond),
            (store_h, store), (heads_h, heads), (source_h, source),
        ],
    )
    loads.wait(0, 1, 2)
    value = active[...].astype(F32)
    for l in range(4):
        act4[pl.ds(128 * l, 128), :] = value
    loads.wait(3, 4, 5, 6)
    condense(
        lambda t: cond[rows(t), :],
        lambda t: store[rows(t), :],
        lambda t: store[rows(t), :] * heads[rows(t), :] + source[rows(t), :],
        act4,
        weights(scale, window),
        copies,
        kept, kept_h, pay, pay_h, sems,
    )


def condense_y_kernel(
    copies, scale_h, window_h, cot_h, cond_h, store_h, active_h,
    kept_h, pay_h,
    scale, window, cot, cond, store, active, act4, cot_t, cond_t, store_t, kept, pay, sems,
):
    loads = Copies(
        sems,
        0,
        [
            (active_h, active), (cond_h, cond), (store_h, store), (cot_h, cot),
            (scale_h, scale), (window_h, window),
        ],
    )
    loads.wait(0)
    value = active[...].astype(F32).T
    for l in range(4):
        act4[pl.ds(128 * l, 128), :] = value
    loads.wait(1)
    transpose_layers(cond, cond_t)
    loads.wait(2)
    transpose_layers(store, store_t)
    loads.wait(3)
    transpose_layers(cot, cot_t)
    loads.wait(4, 5)
    condense(
        lambda t: cond_t[rows(t), :],
        lambda t: store_t[rows(t), :],
        lambda t: cot_t[rows(t), :],
        act4,
        weights(scale, window),
        copies,
        kept, kept_h, pay, pay_h, sems,
    )


def arrivals(size, payloads, got):
    place = lax.axis_index("gx")
    core = lax.rem(place, 2)
    chip = place // 2
    chips = len(payloads)
    pairs = []
    for r, payload in enumerate(payloads):
        first = lax.rem(chip + (chips - r), chips) * 2
        for half, c in enumerate((core, 1 - core)):
            at = pl.multiple_of((first + c) * size, 8)
            pairs.append((payload.at[pl.ds(half * size, size)], got.at[pl.ds(at, size)]))
    return pairs


def middle_x_kernel(count, copies, *refs):
    payloads, refs = refs[: count // 2], refs[count // 2 :]
    (kept_x_h, kept_y_h, chain_h, mid_h, part_h, pay_h,
     got, kept_x, store, kept_y, chain, mid, part, pay, value, links, plain, turned, sems) = refs
    loads = Copies(
        sems,
        0,
        arrivals(32, payloads, got)
        + [
            (kept_x_h.at[pl.ds(LO, 3)], kept_x),
            (kept_x_h.at[STORE], store),
            (kept_y_h.at[pl.ds(INV, 3)], kept_y),
        ],
    )
    loads.wait(*range(count))
    place = lax.axis_index("gx")
    chain_all(got, count, 32, chain, value, links)
    chain[0, 0] = links[place]
    loads.wait(count, count + 1)

    def emit(t, slab):
        mid[t] = slab
        if t < STEPS:
            plain[rows(t), :] = store[t] * slab

    expand(place, count, value, (kept_x.at[0], kept_x.at[1]), kept_x.at[2], emit)
    first = Copies(sems, count + 3, [(chain, chain_h), (mid, mid_h)])
    transpose_layers(plain, turned)
    loads.wait(count + 2)
    condense_right(
        lambda t: turned[rows(t), :], (kept_y.at[1], kept_y.at[2], kept_y.at[0]), part, pay, copies
    )
    second = Copies(sems, count + 5, [(pay, pay_h), (part, part_h)])
    first.wait(0, 1)
    second.wait(0, 1)


def middle_y_kernel(
    count, copies, got_h, kept_y_h, kept_x_h,
    chain_h, adjoint_h, part_h, pay_h,
    got, kept_y, kept_x, chain, adjoint, part, pay, value, links, plain, turned, sems,
):
    loads = Copies(
        sems,
        0,
        [
            (got_h, got),
            (kept_y_h.at[pl.ds(LO, 3)], kept_y),
            (kept_x_h.at[pl.ds(STORE, 4)], kept_x),
        ],
    )
    place = lax.axis_index("gy")
    loads.wait(0)
    chain_all(got, count, 32, chain, value, links)
    chain[0, 0] = links[place]
    first = Copies(sems, 3, [(chain, chain_h)])
    loads.wait(1)

    def emit(t, slab):
        adjoint[t] = slab
        if t < STEPS:
            plain[rows(t), :] = slab

    expand(place, count, value, (kept_y.at[0], kept_y.at[1]), kept_y.at[2], emit)
    second = Copies(sems, 4, [(adjoint, adjoint_h)])
    transpose_layers(plain, turned)
    loads.wait(2)
    condense_right(
        lambda t: turned[rows(t), :] * kept_x[0, t],
        (kept_x.at[2], kept_x.at[3], kept_x.at[1]), part, pay, copies,
    )
    third = Copies(sems, 5, [(pay, pay_h), (part, part_h)])
    first.wait(0)
    second.wait(0)
    third.wait(0, 1)


def sensitivity(face, link, first, second, put):
    even = even_rows()
    for t in range(STEPS):
        value = face[t]
        if t == STEPS - 1:
            value = mixed(even, value, link[...])
        put(t, -value * (first[t] - first[t + 1]) * (second[t] - second[t + 1]))


def final_kernel(nx, ny, got_y_h, *refs):
    payloads, refs = refs[: nx // 2], refs[nx // 2 :]
    (chain_y_h, kept_y_h, part_y_h, adjoint_h, chain_x_h, kept_x_h, part_x_h, mid_h,
     heads_h, sens_y_h, grad_h, sens_x_h,
     got_y, chain_y, kept_y, part_y, face_y, adjoint, value_y, field_y, plain, plain2, heads, sens_y,
     got_x, chain_x, kept_x, part_x, front_x, mid, value_x, field_x, grad, sens_x, sems) = refs
    loads_y = Copies(
        sems,
        0,
        [
            (got_y_h, got_y), (chain_y_h, chain_y), (kept_y_h.at[pl.ds(LO, 2)], kept_y),
            (part_y_h, part_y), (kept_y_h.at[FACE], face_y), (adjoint_h, adjoint),
        ],
    )
    loads_x = Copies(
        sems,
        6,
        arrivals(8, payloads, got_x)
        + [
            (chain_x_h, chain_x), (kept_x_h.at[pl.ds(LO, 2)], kept_x), (part_x_h, part_x),
            (kept_x_h.at[pl.ds(FACE, 2)], front_x), (mid_h, mid),
        ],
    )
    after = nx + 11
    place_y, place_x = lax.axis_index("gy"), lax.axis_index("gx")
    loads_y.wait(0, 1)
    chain_right(got_y, ny, chain_y, value_y)
    loads_y.wait(2, 3)

    def emit(t, slab):
        field_y[t] = slab
        if t < STEPS:
            plain[rows(t), :] = slab

    expand(place_y, ny, value_y, (kept_y.at[0], kept_y.at[1]), part_y, emit)
    transpose_layers(plain, heads)
    stores = [Copies(sems, after, [(heads, heads_h)])]
    loads_y.wait(4, 5)

    def put(t, slab):
        plain2[rows(t), :] = slab

    sensitivity(face_y, chain_y.at[0, 0], adjoint, field_y, put)
    transpose_layers(plain2, sens_y)
    stores.append(Copies(sems, after + 1, [(sens_y, sens_y_h)]))
    loads_x.wait(*range(nx + 3))
    chain_right(got_x, nx, chain_x, value_x)
    loads_x.wait(nx + 3, nx + 4)

    def emit_x(t, slab):
        field_x[t] = slab
        if t < STEPS:
            grad[rows(t), :] = front_x[1, t] * slab

    expand(place_x, nx, value_x, (kept_x.at[0], kept_x.at[1]), part_x, emit_x)
    stores.append(Copies(sems, after + 2, [(grad, grad_h)]))

    def put_x(t, slab):
        sens_x[rows(t), :] = slab

    sensitivity(front_x.at[0], chain_x.at[0, 0], field_x, mid, put_x)
    stores.append(Copies(sems, after + 3, [(sens_x, sens_x_h)]))
    for copy in stores:
        copy.wait(0)


def shaped(*shape):
    return jax.ShapeDtypeStruct(shape, F32)


TALL_STEPS = STEPS + 1
TALL = shaped(TALL_STEPS, *SLAB)
TWO = shaped(2, TALL_STEPS, *SLAB)
THREE = shaped(3, TALL_STEPS, *SLAB)
KEPT = shaped(6, TALL_STEPS, *SLAB)
FOUR = shaped(4, TALL_STEPS, *SLAB)
PLAIN = shaped(512, 128)
ONE = shaped(*SLAB)


def call(kernel, name, args, outs, scratch, copies, cycles, limit):
    return pl.pallas_call(
        kernel,
        name=name,
        out_shape=tuple(outs),
        in_specs=[HBM] * len(args),
        out_specs=tuple([HBM] * len(outs)),
        scratch_shapes=[
            pltpu.VMEM(s.shape, s.dtype) if isinstance(s, jax.ShapeDtypeStruct) else s
            for s in scratch
        ]
        + [pltpu.SemaphoreType.DMA((copies,))],
        cost_estimate=pl.CostEstimate(flops=cycles, bytes_accessed=4000000, transcendentals=0),
        compiler_params=pltpu.CompilerParams(vmem_limit_bytes=limit),
    )(*args)


def spread(payload, axis):
    return lax.all_to_all(payload, axis, split_axis=0, concat_axis=0, tiled=True)


def around(payload):
    size = lax.axis_size("gx")
    other = lax.ppermute(payload, "gx", [(i, i ^ 1) for i in range(size)])
    both = jnp.concatenate([payload, other], axis=0)
    return [both] + [
        lax.ppermute(both, "gx", [(i, (i + r) % size) for i in range(size)])
        for r in range(2, size, 2)
    ]


FULL = 60 * 2**20
LIMITS = (56200000, FULL, 56200000)


def on_device(heads, cond_x, cond_y, store, source, cotangent, active, scale, window):
    nx, ny = lax.axis_size("gx"), lax.axis_size("gy")
    heads, cond_x, cond_y, store, source, cotangent = (
        a.reshape(512, 128) for a in (heads, cond_x, cond_y, store, source, cotangent)
    )
    small = [pltpu.SMEM(scale.shape, F32), pltpu.SMEM(window.shape, jnp.int32)]
    flags = jax.ShapeDtypeStruct((128, 128), jnp.int32)
    x_nodes, y_nodes = shaped(2 * nx, *SLAB), shaped(2 * ny, *SLAB)
    x_chain, y_chain = shaped(3, 2 * nx, *SLAB), shaped(3, 2 * ny, *SLAB)
    pay = shaped(32 * ny, 128)
    kept_y, pay_y = call(
        functools.partial(condense_y_kernel, ny),
        "condense_y",
        (scale, window, cotangent, cond_y, store, active),
        [KEPT, pay],
        small + [PLAIN] * 3 + [flags] + [PLAIN] * 4 + [KEPT, pay],
        6,
        4000000,
        FULL,
    )
    got_y = spread(pay_y, "gy")
    pay = shaped(32, 128)
    kept_x, pay_x = call(
        functools.partial(condense_x_kernel, 1),
        "condense_x",
        (scale, window, heads, cond_x, store, source, active, pay_y),
        [KEPT, pay],
        small + [PLAIN] * 4 + [flags, PLAIN, KEPT, pay],
        7,
        4000000,
        FULL,
    )
    got_x = around(pay_x)
    pay = shaped(8 * ny, 128)
    chain_x, mid, part_y, pay_y = call(
        functools.partial(middle_x_kernel, nx, ny),
        "middle_x",
        (*got_x, kept_x, kept_y),
        [x_chain, TALL, TALL, pay],
        [shaped(32 * nx, 128), THREE, TALL, THREE, x_chain, TALL, TALL, pay]
        + [x_nodes, shaped(nx, *SLAB), PLAIN, PLAIN],
        nx + 7,
        2000000,
        LIMITS[0],
    )
    got_y2 = spread(pay_y, "gy")
    chain_y, adjoint, part_x, pay_x = call(
        functools.partial(middle_y_kernel, ny, 1),
        "middle_y",
        (got_y, kept_y, kept_x),
        [y_chain, TALL, TALL, ONE],
        [shaped(32 * ny, 128), THREE, FOUR, y_chain, TALL, TALL, ONE]
        + [y_nodes, shaped(ny, *SLAB), PLAIN, PLAIN],
        7,
        2000000,
        LIMITS[1],
    )
    got_x2 = around(pay_x)
    new_heads, sens_y, grad, sens_x = call(
        functools.partial(final_kernel, nx, ny),
        "final",
        (got_y2, *got_x2, chain_y, kept_y, part_y, adjoint, chain_x, kept_x, part_x, mid),
        [PLAIN] * 4,
        [shaped(8 * ny, 128), y_chain, TWO, TALL, TALL, TALL, y_nodes, TALL] + [PLAIN] * 4
        + [shaped(8 * nx, 128), x_chain, TWO, TALL, TWO, TALL, x_nodes, TALL] + [PLAIN] * 2,
        nx + 15,
        3000000,
        LIMITS[2],
    )
    return tuple(a.reshape(4, 128, 128) for a in (new_heads, grad, sens_x, sens_y))


def solution(mesh):
    field = P(None, "gx", "gy")
    return jax.shard_map(
        on_device,
        mesh=mesh,
        in_specs=(field,) * 6 + (P("gx", "gy"), P(), P()),
        out_specs=(field,) * 4,
        check_vma=False,
    )
```
